256 devices in a mesh: gx: 4 (over z_lo, core), gy: 4 (over z_hi), gz: 16 (over y, x).
Axes of the slice: x: 4, y: 4, z: 8 (z_hi: 4, z_lo: 2; z = z_hi * 2 + z_lo), core: 2. Of those that a mesh axis runs over, the one named last changes fastest.
Arguments:
- parts: float32 [52, 52, 112, 128], P('gx', 'gy', 'gz'), may hold values from -6 to 6
- cell_matrix: bfloat16 [343, 343], replicated, may hold values from -0.2 to 2
- cell_potential: float32 [343, 8, 8, 16], P(None, 'gx', 'gy', 'gz'), may hold values from 0 to 1
- projectors: bfloat16 [4, 4, 16, 343, 1536], P('gx', 'gy', 'gz'), may hold values from -0.15625 to 0.15625
- slot_atom: int32 [4, 4, 16, 32], P('gx', 'gy'), may hold values from -1 to 63, as said below
- slot_cells: int32 [4, 4, 16, 32, 4], P('gx', 'gy', 'gz'), may hold values from 0 to 3
- coupling: float32 [1024, 12, 12], P(('gx', 'gy')), may hold values from -1.75 to 1.75
Outputs:
- filtered: float32 [52, 52, 112, 128], P('gx', 'gy', 'gz')
The draws below stay inside these ranges and needn't reach their ends.
Inputs may be any that keep to these rules, and one draw needn't show every extreme that they name: `slot_atom`: entry s of partition (i, j, k) is -1 (an empty slot) or the number, within the column (i, j), of an atom whose projectors reach into that partition. Slots c * 2 to c * 2 + 1 of every partition hold only atoms numbered c * 4 to c * 4 + 3, which are owned by partition c of the column along gz. An atom stands at most once in one partition's list.
All inputs are finite; a program needn't handle non-finite values.
Results may differ from the reference program's by a relative error of at most 0.0058.
Values may be sent and summed in bfloat16 or wider, within the bound.
A program may use at most 64 MiB of HBM per device.

```python
import jax
import jax.numpy as jnp
from jax import lax

ORB = 128
ORDER = 6
CX = 2
CY = 2
CZ = 1
STEPS = 3
PA = 12
POS = 32
BLK = 4
CELL_NODES = 343
NXD = 13
NYD = 13
NZD = 7
NCX = 8
NCY = 8
NCZ = 16
CELLS = 4
CAP = 2
OWN = 4
COL_ATOMS = 64
ATOMS_ALL = 1024
PROJ_COLS = 1536
N_GX = 4
N_GY = 4
N_GZ = 16


def draw_slot_atom(key, part):
    columns = N_GX * N_GY
    first_key, second_key, third_key = jax.random.split(key, 3)
    busy_owner = jax.random.randint(first_key, (columns,), 0, N_GZ)
    filled = jax.random.randint(second_key, (columns, N_GZ, N_GZ), 0, CAP + 1)
    owners = jnp.arange(N_GZ)[None, None, :]
    sources = jnp.arange(N_GZ)[None, :, None]
    busy_mask = owners == busy_owner[:, None, None]
    filled = jnp.where(busy_mask, CAP, filled)
    filled = jnp.where(sources == 0, jnp.maximum(filled, 1), filled)
    spare_owner = (busy_owner + 1) % N_GZ
    spare_mask = (owners == spare_owner[:, None, None]) & (sources == N_GZ - 1)
    filled = jnp.where(spare_mask, jnp.minimum(filled, CAP - 1), filled)
    local_numbers = jnp.arange(OWN)
    scores = jax.random.randint(third_key, (columns, N_GZ, N_GZ, OWN), 0, 1 << 20) * OWN + local_numbers
    forced = (sources[..., None] == 0) & (local_numbers == OWN - 1)
    scores = jnp.where(forced, -1, scores)
    ranked = jnp.argsort(scores, axis=-1)[..., :CAP]
    atom_number = owners[..., None] * OWN + ranked
    occupied = jnp.arange(CAP)[None, None, None, :] < filled[..., None]
    atom_ids = jnp.where(occupied, atom_number, -1)
    return atom_ids.reshape(N_GX, N_GY, N_GZ, POS).astype(jnp.int32)


def draw_cell_matrix(key, part):
    edge_nodes = ORDER + 1
    cell_nodes = edge_nodes ** 3
    first_key, second_key = jax.random.split(key)
    coupling_part = jnp.clip(jax.random.normal(first_key, (cell_nodes, cell_nodes), jnp.float32), -4.0, 4.0)
    diagonal = jax.random.uniform(second_key, (cell_nodes,), jnp.float32, 1.2, 1.8)
    symmetric = (coupling_part + coupling_part.T) * (0.5 / (2.0 * cell_nodes) ** 0.5)
    edge_index = jnp.arange(edge_nodes)
    line_weight = jnp.where((edge_index == 0) | (edge_index == edge_nodes - 1), 2.0, 1.0)
    multiplicity = (line_weight[:, None, None] * line_weight[None, :, None] * line_weight[None, None, :]).reshape(cell_nodes)
    root_weight = jnp.sqrt(multiplicity)
    identity = jnp.eye(cell_nodes, dtype=jnp.float32)
    off_diagonal = symmetric * (1.0 - identity) / (root_weight[:, None] * root_weight[None, :])
    matrix = off_diagonal + identity * (diagonal / multiplicity)[:, None]
    return matrix.astype(jnp.bfloat16)


def touch_ends(values, rng, low, largest):
    longest = values.shape.index(max(values.shape))
    spots = []
    for shift in (0, 1):
        where = [jax.random.randint(jax.random.fold_in(rng, axis), (), 0, length) for axis, length in enumerate(values.shape)]
        where[longest] = (where[longest] + shift) % values.shape[longest]
        spots.append(tuple(where))
    return values.at[spots[0]].set(low).at[spots[1]].set(largest)


def block_levels(key, shape, shards, least, largest):
    def one(axis_at, blocks):
        steps = jax.random.uniform(jax.random.fold_in(jax.random.fold_in(key, 6), axis_at), (blocks,), jnp.float32, least / len(shards), largest / len(shards))
        return jnp.repeat(jnp.exp(steps), shape[axis_at] // blocks).reshape((-1,) + (1,) * (len(shape) - axis_at - 1))

    loudness = one(*shards[0])
    for cut in shards[1:]:
        loudness = loudness * one(*cut)
    return loudness


def bell_draw(key, extent, scale, limit, cuts=(), kind=jnp.bfloat16):
    entries = jax.random.normal(key, extent, jnp.float32) * scale
    if len(cuts) > 0:
        entries = block_levels(key, extent, cuts, -0.22, 0.18) * entries
    return jnp.clip(entries, min=-limit, max=limit).astype(kind)


def setup_inputs(seed: int = 0) -> dict:
    streams_of = jax.random.split(jax.random.key(seed), 8)
    return {
        "parts": bell_draw(streams_of[0], (N_GX * NXD, N_GY * NYD, N_GZ * NZD, ORB), 1.0, 6.0, ((0, 4), (1, 4), (2, 16)), jnp.float32),
        "cell_matrix": draw_cell_matrix(jax.random.fold_in(streams_of[7], 71), 0),
        "cell_potential": jnp.clip(1.0 * jax.random.uniform(streams_of[2], (CELL_NODES, NCX, NCY, NCZ), jnp.float32) ** block_levels(streams_of[2], (CELL_NODES, NCX, NCY, NCZ), ((1, 4), (2, 4), (3, 16)), -0.2, 0.2), 0.0, 1.0),
        "projectors": bell_draw(streams_of[3], (N_GX, N_GY, N_GZ, CELL_NODES, PROJ_COLS), (BLK * CELL_NODES) ** -0.5, 0.15625, ((0, 4), (1, 4), (2, 16))),
        "slot_atom": draw_slot_atom(jax.random.fold_in(streams_of[7], 71), 0),
        "slot_cells": touch_ends(jax.random.randint(streams_of[5], (N_GX, N_GY, N_GZ, POS, BLK), 0, CELLS), jax.random.fold_in(streams_of[5], 1), 0, CELLS - 1).astype(jnp.int32),
        "coupling": bell_draw(streams_of[6], (ATOMS_ALL, PA, PA), PA ** -0.5, 1.75, ((0, 16),), jnp.float32),
    }


center_value = 2.0
half_width = 3.0


def split_axis(values, which_axis, number, stride):
    rotated = jnp.moveaxis(values, which_axis, 0)
    leading = rotated[:number * stride].reshape((number, stride) + rotated.shape[1:])
    closing = rotated[stride::stride][:, None]
    blocks = jnp.concatenate([leading, closing], axis=1)
    return jnp.moveaxis(blocks, (0, 1), (which_axis, which_axis + 1))


def join_axis(blocks, which_axis, stride):
    rotated = jnp.moveaxis(blocks, (which_axis, which_axis + 1), (0, 1))
    number = rotated.shape[0]
    remaining = rotated.shape[2:]
    leading = rotated[:, :stride].reshape((number * stride,) + remaining)
    final_layer = rotated[:, stride]
    empty_row = jnp.zeros((1,) + remaining, rotated.dtype)
    primary = jnp.concatenate([leading, empty_row], axis=0)
    trailing = jnp.concatenate([jnp.zeros((number, stride - 1) + remaining, rotated.dtype), final_layer[:, None]], axis=1)
    appended = jnp.concatenate([empty_row, trailing.reshape((number * stride,) + remaining)], axis=0)
    return jnp.moveaxis(primary + appended, 0, which_axis)


def cell_values(values, cell_counts):
    blocks = split_axis(values, 0, cell_counts[0], ORDER)
    blocks = split_axis(blocks, 2, cell_counts[1], ORDER)
    blocks = split_axis(blocks, 4, cell_counts[2], ORDER)
    blocks = jnp.transpose(blocks, (1, 3, 5, 0, 2, 4, 6))
    edge_nodes = ORDER + 1
    return blocks.reshape(edge_nodes ** 3, cell_counts[0] * cell_counts[1] * cell_counts[2], blocks.shape[-1])


def assemble(cell_data, cell_counts):
    edge_nodes = ORDER + 1
    blocks = cell_data.reshape((edge_nodes, edge_nodes, edge_nodes, cell_counts[0], cell_counts[1], cell_counts[2], cell_data.shape[-1]))
    blocks = jnp.transpose(blocks, (3, 0, 4, 1, 5, 2, 6))
    blocks = join_axis(blocks, 4, ORDER)
    blocks = join_axis(blocks, 2, ORDER)
    return join_axis(blocks, 0, ORDER)


def device_major(cell_data):
    cell_nodes, total_cells, orbitals = cell_data.shape
    arranged = cell_data.reshape(cell_nodes, N_GX, CX, N_GY, CY, N_GZ, CZ, orbitals)
    arranged = jnp.transpose(arranged, (1, 3, 5, 0, 2, 4, 6, 7))
    return arranged.reshape(N_GX * N_GY * N_GZ, cell_nodes, CX * CY * CZ, orbitals)


def cell_major(blocks):
    devices, cell_nodes, number, orbitals = blocks.shape
    arranged = blocks.reshape(N_GX, N_GY, N_GZ, cell_nodes, CX, CY, CZ, orbitals)
    arranged = jnp.transpose(arranged, (3, 0, 4, 1, 5, 2, 6, 7))
    return arranged.reshape(cell_nodes, N_GX * CX * N_GY * CY * N_GZ * CZ, orbitals)


def reference(parts, cell_matrix, cell_potential, projectors, slot_atom, slot_cells, coupling):
    devices = N_GX * N_GY * N_GZ
    cell_counts = (CX * N_GX, CY * N_GY, CZ * N_GZ)
    cell_nodes = cell_matrix.shape[0]
    orbitals = parts.shape[-1]
    blocks = parts.reshape(N_GX, NXD, N_GY, NYD, N_GZ, NZD, orbitals)
    assembled = join_axis(blocks, 4, ORDER * CZ)
    assembled = join_axis(assembled, 2, ORDER * CY)
    assembled = join_axis(assembled, 0, ORDER * CX)
    projector_cols = projectors.reshape(devices, cell_nodes, POS * BLK, PA)
    cell_index = slot_cells.reshape(devices, POS * BLK)
    column = jnp.arange(devices, dtype=jnp.int32) // N_GZ
    atom_ids = slot_atom.reshape(devices, POS)
    atom_count = coupling.shape[0]
    global_ids = jnp.where(atom_ids >= 0, column[:, None] * COL_ATOMS + atom_ids, atom_count).astype(jnp.int32)
    potential = device_major(cell_potential.reshape(cell_nodes, -1, 1))[..., 0]

    def apply_hamiltonian(values):
        cell_data = device_major(cell_values(values, cell_counts))

        def project_slots(inputs):
            cells_dev, proj_dev, index_dev = inputs
            picked = jnp.take(cells_dev.astype(jnp.bfloat16), index_dev, axis=1).astype(jnp.float32)
            products = jnp.einsum('nqa,nqo->qao', proj_dev.astype(jnp.float32), picked)
            return products.reshape(POS, BLK, PA, orbitals).sum(axis=1)

        partials = lax.map(project_slots, (cell_data, projector_cols, cell_index))
        totals = jax.ops.segment_sum(partials.reshape(devices * POS, PA, orbitals), global_ids.reshape(-1), num_segments=atom_count + 1)[:atom_count]
        coupled = jnp.einsum('tab,tbo->tao', coupling, totals, precision=lax.Precision.HIGHEST)
        coefficient = jnp.concatenate([coupled.astype(jnp.bfloat16), jnp.zeros((1, PA, orbitals), jnp.bfloat16)], axis=0)
        slot_coef = coefficient[global_ids]

        def cell_work(inputs):
            cells_dev, potential_dev, proj_dev, index_dev, coef_dev = inputs
            cell_bf = cells_dev.astype(jnp.bfloat16)
            stiffness = jnp.dot(cell_matrix, cell_bf.reshape(cell_nodes, -1), preferred_element_type=jnp.float32).reshape(cells_dev.shape)
            stiffness = stiffness + potential_dev[:, :, None] * cells_dev
            spread = jnp.broadcast_to(coef_dev[:, None], (POS, BLK, PA, orbitals)).reshape(POS * BLK, PA, orbitals)
            contribution = jnp.einsum('nqa,qao->nqo', proj_dev.astype(jnp.float32), spread.astype(jnp.float32))
            return stiffness.at[:, index_dev].add(contribution)

        result = lax.map(cell_work, (cell_data, potential, projector_cols, cell_index, slot_coef))
        return assemble(cell_major(result), cell_counts)

    previous = assembled
    current = (apply_hamiltonian(assembled) - center_value * assembled) / half_width
    for degree in range(1, STEPS):
        following = 2.0 * (apply_hamiltonian(current) - center_value * current) / half_width - previous
        previous, current = current, following
    output = split_axis(current, 0, N_GX, ORDER * CX)
    output = split_axis(output, 2, N_GY, ORDER * CY)
    output = split_axis(output, 4, N_GZ, ORDER * CZ)
    return output.reshape(N_GX * NXD, N_GY * NYD, N_GZ * NZD, orbitals)
```

```python
import jax
import jax.numpy as jnp
from jax import lax
from jax.experimental import pallas as pl
from jax.experimental.pallas import tpu as pltpu
from jax.sharding import PartitionSpec as P

ORDER = 6
STEPS = 3
PA = 12
POS = 32
BLK = 4
CELLS = 4

EDGE = ORDER + 1
NODES = EDGE**3
WIDE = 2 * ORDER + 1
SUB = 8
LANES = 128
ROW = WIDE * SUB
FIELD = WIDE * ROW
TALL = 1408
CROWS = 400
KPAD = 512
SLOT = 16
COLS = POS * SLOT
GROUP = 8 * SLOT
PGROUP = 8 * BLK * PA

center_value = 2.0
half_width = 3.0

MESH = pl.DeviceIdType.MESH
BF = jnp.bfloat16
F32 = jnp.float32

FACES = [(1, 0, 0), (-1, 0, 0), (0, 1, 0), (0, -1, 0), (0, 0, 1), (0, 0, -1)]
XY = [(a, b, 0) for a in (-1, 1) for b in (-1, 1)]
XZ = [(a, 0, b) for a in (-1, 1) for b in (-1, 1)]
YZ = [(0, a, b) for a in (-1, 1) for b in (-1, 1)]
CORNERS = [(a, b, c) for a in (-1, 1) for b in (-1, 1) for c in (-1, 1)]
DIRS = CORNERS + XY + YZ + FACES + XZ


def region_rows(d):
    if d[2] != 0 and d[0] == 0 and d[1] == 0:
        return 176
    if sum(1 for x in d if x != 0) == 1:
        return 112
    return 16


OFFSET = {}
_total = 0
for _d in DIRS:
    OFFSET[_d] = _total
    _total += region_rows(_d)
HALO_ROWS = _total


def side(step, last):
    return last if step > 0 else 0


def iota(shape, axis):
    return lax.broadcasted_iota(jnp.int32, shape, axis)


def dot(a, b):
    return jnp.dot(a, b, preferred_element_type=F32)


def dot_nt(a, b):
    return lax.dot_general(a, b, (((1,), (1,)), ((), ())), preferred_element_type=F32)


def onehot(mask):
    return jnp.where(mask, 1.0, 0.0).astype(BF)


def body(sizes, parts, amat, pot, proj, atoms, cells, coup, out,
         zbuf, field, ybuf, xcat, qt, q, a2, vloc, gmat, csc,
         part_send, part_recv, coef_send, coef_recv, halo_send, halo_recv,
         hsend_sem, hrecv_sem, psend_sem, precv_sem, csend_sem, crecv_sem):
    ngx, ngy, ngz = sizes
    ix, iy, iz = lax.axis_index("gx"), lax.axis_index("gy"), lax.axis_index("gz")
    cap = POS // ngz
    own = coup.shape[0] // ngz
    chunk = cap * SLOT

    def exists(d, sign):
        ok = None
        for pos, size, step in ((ix, ngx, d[0]), (iy, ngy, d[1]), (iz, ngz, d[2])):
            if step == 0:
                continue
            c = (pos + 1 < size) if step * sign > 0 else (pos > 0)
            ok = c if ok is None else jnp.logical_and(ok, c)
        return ok

    def target(d):
        return (ix + d[0], iy + d[1], iz + d[2])

    def peer(k):
        return lax.rem(iz + k, ngz)

    halo_recv[...] = jnp.zeros(halo_recv.shape, BF)
    barrier = pltpu.get_barrier_semaphore()
    for d in DIRS:
        @pl.when(exists(d, 1))
        def _(d=d):
            pl.semaphore_signal(barrier, inc=1, device_id=target(d), device_id_type=MESH)

    def greet(k, carry):
        pl.semaphore_signal(barrier, inc=1, device_id=(ix, iy, peer(k)), device_id_type=MESH)
        return carry

    lax.fori_loop(1, ngz, greet, 0)

    def span(pos, size):
        return 1 + (pos > 0).astype(jnp.int32) + (pos + 1 < size).astype(jnp.int32)

    n_greet = span(ix, ngx) * span(iy, ngy) * span(iz, ngz) - 1 + ngz - 1

    zero8 = jnp.zeros((SUB, LANES), F32)
    field[FIELD:, :] = jnp.zeros((TALL - FIELD, LANES), F32)
    ybuf[...] = jnp.zeros(ybuf.shape, F32)

    def take(u, carry):
        for v in range(WIDE):
            at = pl.multiple_of(u * ROW, SUB) + v * SUB
            tile = jnp.concatenate([parts[u, v], jnp.zeros((1, LANES), F32)], axis=0)
            field[pl.ds(at, SUB), :] = tile
        return carry

    lax.fori_loop(0, WIDE, take, 0)

    def halo_copy(d, slot):
        source = (d[0], d[1], 0) if d in CORNERS else d
        n = region_rows(d)
        k = DIRS.index(d)
        return pltpu.make_async_remote_copy(
            src_ref=halo_send.at[pl.ds(OFFSET[source], n)],
            dst_ref=halo_recv.at[slot, pl.ds(OFFSET[d], n)],
            send_sem=hsend_sem.at[k],
            recv_sem=hrecv_sem.at[slot, k],
            device_id=target(d),
            device_id_type=MESH,
        )

    def pack():
        def put(d, value):
            halo_send[pl.ds(OFFSET[d], region_rows(d)), :] = value.astype(BF)

        for d in XY:
            at = side(d[0], WIDE - 1) * ROW + side(d[1], WIDE - 1) * SUB
            put(d, jnp.concatenate([field[pl.ds(at, SUB), :], zero8], axis=0))
        for d in FACES:
            if d[0] != 0:
                at = side(d[0], WIDE - 1) * ROW
                put(d, jnp.concatenate([field[pl.ds(at, ROW), :], zero8], axis=0))
            elif d[1] != 0:
                v = side(d[1], WIDE - 1)
                value = jnp.concatenate(
                    [field[pl.ds(u * ROW + v * SUB, SUB), :] for u in range(WIDE)], axis=0)
                ybuf[pl.ds(side(d[1], 1) * LANES, ROW), :] = value
                put(d, jnp.concatenate([value, zero8], axis=0))
            else:
                put(d, field[pl.ds(side(d[2], ORDER), 176, stride=SUB), :])
        for d in YZ:
            put(d, ybuf[pl.ds(side(d[1], 1) * LANES + side(d[2], ORDER), 16, stride=SUB), :])
        for d in XZ:
            at = side(d[0], WIDE - 1) * ROW + side(d[2], ORDER)
            put(d, field[pl.ds(at, 16, stride=SUB), :])

    def halo_start(slot):
        for d in DIRS:
            @pl.when(exists(d, 1))
            def _(d=d):
                halo_copy(d, slot).start()

    def halo_wait(slot):
        for d in DIRS:
            @pl.when(exists(d, -1))
            def _(d=d):
                halo_copy(d, slot).wait_recv()
        for d in DIRS:
            @pl.when(exists(d, 1))
            def _(d=d):
                halo_copy(d, slot).wait_send()

    def unpack(slot):
        def got(d):
            return halo_recv[slot, pl.ds(OFFSET[d], region_rows(d)), :].astype(F32)

        def other(step, last):
            return 0 if step > 0 else last

        keep = iota((16, LANES), 0) < WIDE
        for d in FACES:
            if d[0] != 0:
                at = pl.ds(other(d[0], WIDE - 1) * ROW, ROW)
                field[at, :] = field[at, :] + got(d)[:ROW]
            elif d[1] != 0:
                v = other(d[1], WIDE - 1)
                ybuf[pl.ds(0, ROW), :] = got(d)[:ROW]
                for dz in (-1, 1):
                    rows = pl.ds(other(dz, ORDER), 16, stride=SUB)
                    ybuf[rows, :] = ybuf[rows, :] + got((0, d[1], dz))
                for u in range(WIDE):
                    at = pl.ds(u * ROW + v * SUB, SUB)
                    field[at, :] = field[at, :] + ybuf[pl.ds(u * SUB, SUB), :]
            else:
                rows = pl.ds(other(d[2], ORDER), 176, stride=SUB)
                field[rows, :] = field[rows, :] + got(d)
        for d in XZ:
            rows = pl.ds(other(d[0], WIDE - 1) * ROW + other(d[2], ORDER), 16, stride=SUB)
            field[rows, :] = field[rows, :] + jnp.where(keep, got(d), 0.0)
        for d in XY:
            base = other(d[0], WIDE - 1) * ROW + other(d[1], WIDE - 1) * SUB
            at = pl.ds(base, SUB)
            total = field[at, :] + got(d)[:SUB]
            field[at, :] = total
            first = got((d[0], d[1], 1))[ORDER:EDGE]
            last = got((d[0], d[1], -1))[:1]
            field[pl.ds(base, 1), :] = field[pl.ds(base, 1), :] + first
            field[pl.ds(base + ORDER, 1), :] = field[pl.ds(base + ORDER, 1), :] + last

    def split_cells(values):
        xs = []
        for p in range(2):
            for r in range(2):
                pieces = [
                    values[(ORDER * p + a) * ROW + ORDER * SUB * r:
                           (ORDER * p + a) * ROW + ORDER * SUB * r + EDGE * SUB]
                    for a in range(EDGE)]
                xs.append(jnp.concatenate(pieces + [zero8], axis=0))
        return xs

    def join_cells(blocks):
        rows = []
        for u in range(WIDE):
            halves = []
            for r in range(2):
                value = None
                for p in range(2):
                    a = u - ORDER * p
                    if 0 <= a <= ORDER:
                        piece = blocks[2 * p + r][a * EDGE * SUB:(a + 1) * EDGE * SUB]
                        value = piece if value is None else value + piece
                halves.append(value)
            left, right = halves
            cut = ORDER * SUB
            rows.append(jnp.concatenate(
                [left[:cut], left[cut:] + right[:SUB], right[SUB:]], axis=0))
        return rows

    pack()
    pl.semaphore_wait(barrier, n_greet)
    halo_start(0)

    r_i, n_i = iota((KPAD, NODES), 0), iota((KPAD, NODES), 1)
    expand = onehot(jnp.logical_and(
        jnp.logical_and(r_i < EDGE * EDGE * SUB, (r_i & 7) < EDGE),
        n_i == (r_i >> 3) * EDGE + (r_i & 7)))
    short = expand[:CROWS]
    a2[...] = dot_nt(dot(short, amat[...]).astype(BF), expand).astype(BF)

    wide_pot = jnp.concatenate(
        [jnp.broadcast_to(pot[:, g:g + 1], (NODES, LANES)) for g in range(CELLS)], axis=1)
    v_cells = jnp.dot(short.astype(F32), wide_pot, precision=lax.Precision.HIGHEST,
                      preferred_element_type=F32)
    for u, row in enumerate(join_cells(
            [v_cells[:, g * LANES:(g + 1) * LANES] for g in range(CELLS)])):
        vloc[pl.ds(u * ROW, ROW), :] = row

    width = POS * BLK * PA
    s_i, col = iota((POS, width), 0), iota((POS, width), 1)
    cell_f = cells[...].astype(F32)
    cell_col = jnp.zeros((1, width), F32)
    for b in range(BLK):
        start = s_i * (BLK * PA) + b * PA
        inside = jnp.logical_and(col >= start, col < start + PA)
        cell_col = cell_col + jnp.sum(
            jnp.where(inside, jnp.broadcast_to(cell_f[:, b:b + 1], (POS, width)), 0.0),
            axis=0, keepdims=True)
    in_slot = onehot(jnp.logical_and(col >= s_i * (BLK * PA), col < (s_i + 1) * (BLK * PA)))
    atom_bf = atoms[...].astype(F32).astype(BF)
    atom_all = dot(atom_bf, in_slot)
    atom_col = jnp.sum(jnp.where(iota((ngz, width), 0) == iz, atom_all, 0.0),
                       axis=0, keepdims=True)

    wide_proj = dot(expand, proj[...])
    rr, rc = iota((PGROUP, GROUP), 0), iota((PGROUP, GROUP), 1)
    tr, tc = iota((GROUP, PGROUP), 1), iota((GROUP, PGROUP), 0)

    def merge(row, column):
        base = (column >> 4) * (BLK * PA) + (column & 15)
        hit = row == base
        for b in range(1, BLK):
            hit = jnp.logical_or(hit, row == base + b * PA)
        return onehot(jnp.logical_and(hit, (column & 15) < PA))

    narrow, narrow_t = merge(rr, rc), merge(tr, tc)
    for g in range(CELLS):
        live = jnp.logical_and(cell_col == g, atom_col >= 0.0)
        masked = jnp.where(live, wide_proj, 0.0).astype(BF)
        for k in range(POS // 8):
            piece = masked[:, k * PGROUP:(k + 1) * PGROUP]
            q[pl.ds(g * CROWS, CROWS), pl.ds(k * GROUP, GROUP)] = dot(
                piece[:CROWS], narrow).astype(BF)
            qt[pl.ds(k * GROUP, GROUP), pl.ds(g * KPAD, KPAD)] = dot_nt(
                narrow_t, piece).astype(BF)

    at_s, at_c = iota((POS, COLS), 0), iota((POS, COLS), 1)
    j_c = lax.rem(at_c >> 4, cap)
    src = onehot(at_s == iz * cap + j_c)
    got_atoms = dot(atom_bf, src)
    k_r, k_c = iota((ngz, COLS), 0), iota((ngz, COLS), 1)
    here = jnp.logical_and(k_c >= k_r * chunk, k_c < (k_r + 1) * chunk)
    atom_row = jnp.sum(jnp.where(here, got_atoms, 0.0), axis=0, keepdims=True)
    m_r, m_c = iota((LANES, COLS), 0), iota((LANES, COLS), 1)
    same = jnp.logical_and((m_r & 15) == (m_c & 15), (m_r & 15) < PA)
    number = (m_r >> 4).astype(F32)
    base_atom = (iz * own).astype(F32)
    member = onehot(jnp.logical_and(
        same, jnp.broadcast_to(atom_row, (LANES, COLS)) - base_atom == number))
    member_t = dot_nt(onehot(iota((COLS, COLS), 0) == iota((COLS, COLS), 1)),
                      member).astype(BF)
    csc[...] = jnp.zeros(csc.shape, F32)
    for m in range(own):
        csc[pl.ds(m * SLOT, PA), pl.ds(0, PA)] = coup[iz * own + m]
    c_r, c_c = iota((LANES, LANES), 0), iota((LANES, LANES), 1)
    spread = onehot(jnp.logical_and(c_r == (c_c & 15), (c_c & 15) < PA))
    diagonal = (c_r >> 4) == (c_c >> 4)
    whole = csc[...]
    high = whole.astype(BF)
    low = (whole - high.astype(F32)).astype(BF)
    for h, piece in enumerate((high, low)):
        block = jnp.where(diagonal, dot(piece, spread), 0.0).astype(BF)
        gmat[h] = dot(dot(member_t, block).astype(BF), member).astype(BF)

    xcat[CROWS:, :] = jnp.zeros((KPAD - CROWS, CELLS * LANES), BF)
    zbuf[1] = jnp.zeros((FIELD, LANES), F32)

    halo_wait(0)
    unpack(0)
    zbuf[0] = field[pl.ds(0, FIELD), :]
    for g, value in enumerate(split_cells(field[pl.ds(0, FIELD), :])):
        xcat[pl.ds(0, CROWS), pl.ds(g * LANES, LANES)] = value.astype(BF)

    def exchange(src, dst, send_sem, recv_sem, k):
        to = peer(k)
        return pltpu.make_async_remote_copy(
            src_ref=src.at[pl.ds(pl.multiple_of(to * chunk, chunk), chunk)],
            dst_ref=dst.at[pl.ds(pl.multiple_of(iz * chunk, chunk), chunk)],
            send_sem=send_sem.at[k],
            recv_sem=recv_sem.at[k],
            device_id=(ix, iy, to),
            device_id_type=MESH,
        )

    def start_all(src, dst, send_sem, recv_sem):
        def go(k, carry):
            exchange(src, dst, send_sem, recv_sem, k).start()
            return carry

        lax.fori_loop(1, ngz, go, 0)
        mine = pl.ds(pl.multiple_of(iz * chunk, chunk), chunk)
        dst[mine, :] = src[mine, :]

    def wait_all(src, dst, send_sem, recv_sem):
        def go(k, carry):
            exchange(src, dst, send_sem, recv_sem, k).wait()
            return carry

        lax.fori_loop(1, ngz, go, 0)

    def step(t, carry):
        slot = lax.rem(t + 1, 2)
        now = lax.rem(t, 2)
        scale = jnp.where(t == 0, 1.0, 2.0) / half_width

        total = None
        for g in range(CELLS):
            term = dot(qt[:, g * KPAD:(g + 1) * KPAD], xcat[:, g * LANES:(g + 1) * LANES])
            total = term if total is None else total + term
        part_send[...] = total.astype(BF)
        start_all(part_send, part_recv, psend_sem, precv_sem)

        stiff = dot(a2[...], xcat[...])
        rows = join_cells([stiff[:, g * LANES:(g + 1) * LANES] for g in range(CELLS)])
        for u, row in enumerate(rows):
            at = pl.ds(u * ROW, ROW)
            field[at, :] = row + vloc[at, :] * zbuf[now, at, :]

        wait_all(part_send, part_recv, psend_sem, precv_sem)
        received = part_recv[...]
        coef_send[...] = (dot(gmat[0], received) + dot(gmat[1], received)).astype(BF)
        start_all(coef_send, coef_recv, csend_sem, crecv_sem)
        wait_all(coef_send, coef_recv, csend_sem, crecv_sem)

        coef = coef_recv[...]
        spread_cells = [dot(q[pl.ds(g * CROWS, CROWS), :], coef) for g in range(CELLS)]
        for u, row in enumerate(join_cells(spread_cells)):
            at = pl.ds(u * ROW, ROW)
            field[at, :] = field[at, :] + row

        pack()
        halo_start(slot)
        halo_wait(slot)
        unpack(slot)
        new = (field[pl.ds(0, FIELD), :] - center_value * zbuf[now]) * scale - zbuf[slot]
        zbuf[slot] = new
        for g, value in enumerate(split_cells(new)):
            xcat[pl.ds(0, CROWS), pl.ds(g * LANES, LANES)] = value.astype(BF)
        return carry

    lax.fori_loop(0, STEPS, step, 0)

    def give(u, carry):
        for v in range(WIDE):
            at = pl.multiple_of(u * ROW, SUB) + v * SUB
            out[u, v] = zbuf[STEPS % 2, pl.ds(at, SUB), :][:EDGE]
        return carry

    lax.fori_loop(0, WIDE, give, 0)


def local(sizes, parts, cell_matrix, cell_potential, projectors, slot_atom, slot_cells, coupling):
    ngz = sizes[2]

    def kernel(*refs):
        body(sizes, *refs)

    vm = pltpu.VMEM
    dma = pltpu.SemaphoreType.DMA
    n = len(DIRS)
    return pl.pallas_call(
        kernel,
        out_shape=jax.ShapeDtypeStruct(parts.shape, F32),
        in_specs=[pl.BlockSpec(memory_space=pltpu.VMEM)] * 7,
        out_specs=pl.BlockSpec(memory_space=pltpu.VMEM),
        scratch_shapes=[
            vm((2, FIELD, LANES), F32),
            vm((TALL, LANES), F32),
            vm((2 * LANES, LANES), F32),
            vm((KPAD, CELLS * LANES), BF),
            vm((COLS, CELLS * KPAD), BF),
            vm((CELLS * CROWS, COLS), BF),
            vm((CROWS, KPAD), BF),
            vm((FIELD, LANES), F32),
            vm((2, COLS, COLS), BF),
            vm((LANES, LANES), F32),
            vm((COLS, LANES), BF),
            vm((COLS, LANES), BF),
            vm((COLS, LANES), BF),
            vm((COLS, LANES), BF),
            vm((HALO_ROWS, LANES), BF),
            vm((2, HALO_ROWS, LANES), BF),
            dma((n,)),
            dma((2, n)),
            dma((ngz,)),
            dma((ngz,)),
            dma((ngz,)),
            dma((ngz,)),
        ],
        compiler_params=pltpu.CompilerParams(
            collective_id=0, has_side_effects=True, vmem_limit_bytes=56 * 1024 * 1024),
    )(
        parts,
        cell_matrix,
        cell_potential.reshape(NODES, CELLS),
        projectors.reshape(NODES, POS * BLK * PA),
        slot_atom.reshape(ngz, POS),
        slot_cells.reshape(POS, BLK),
        coupling,
    )


def solution(mesh):
    sizes = tuple(mesh.shape[a] for a in ("gx", "gy", "gz"))

    def run(*args):
        return local(sizes, *args)

    in_specs = (
        P("gx", "gy", "gz", None),
        P(),
        P(None, "gx", "gy", "gz"),
        P("gx", "gy", "gz", None, None),
        P("gx", "gy", None, None),
        P("gx", "gy", "gz", None, None),
        P(("gx", "gy"), None, None),
    )
    out_specs = P("gx", "gy", "gz", None)
    return jax.shard_map(run, mesh=mesh, in_specs=in_specs, out_specs=out_specs, check_vma=False)
```

```python
import jax
import jax.numpy as jnp
from jax import lax
from jax.experimental import pallas as pl
from jax.experimental.pallas import tpu as pltpu
from jax.sharding import PartitionSpec as P

ORDER = 6
STEPS = 3
PA = 12
POS = 32
BLK = 4
CELLS = 4

EDGE = ORDER + 1
NODES = EDGE**3
WIDE = 2 * ORDER + 1
SUB = 8
LANES = 128
ROW = WIDE * SUB
FIELD = WIDE * ROW
TALL = 1408
CROWS = 400
KPAD = 512
SLOT = 16
COLS = POS * SLOT
GROUP = 8 * SLOT
PGROUP = 8 * BLK * PA

center_value = 2.0
half_width = 3.0

MESH = pl.DeviceIdType.MESH
BF = jnp.bfloat16
F32 = jnp.float32

FACES = [(1, 0, 0), (-1, 0, 0), (0, 1, 0), (0, -1, 0), (0, 0, 1), (0, 0, -1)]
XY = [(a, b, 0) for a in (-1, 1) for b in (-1, 1)]
XZ = [(a, 0, b) for a in (-1, 1) for b in (-1, 1)]
YZ = [(0, a, b) for a in (-1, 1) for b in (-1, 1)]
CORNERS = [(a, b, c) for a in (-1, 1) for b in (-1, 1) for c in (-1, 1)]
DIRS = CORNERS + XY + YZ + FACES + XZ


def region_rows(d):
    if d[2] != 0 and d[0] == 0 and d[1] == 0:
        return 176
    if sum(1 for x in d if x != 0) == 1:
        return 112
    return 16


OFFSET = {}
_total = 0
for _d in DIRS:
    OFFSET[_d] = _total
    _total += region_rows(_d)
HALO_ROWS = _total


def side(step, last):
    return last if step > 0 else 0


def iota(shape, axis):
    return lax.broadcasted_iota(jnp.int32, shape, axis)


def dot(a, b):
    return jnp.dot(a, b, preferred_element_type=F32)


def dot_nt(a, b):
    return lax.dot_general(a, b, (((1,), (1,)), ((), ())), preferred_element_type=F32)


def onehot(mask):
    return jnp.where(mask, 1.0, 0.0).astype(BF)


def body(sizes, parts_in, amat_in, pot_in, proj_in, atoms_in, cells_in, coup_in, out,
         parts, amat, pot, proj, atoms, cells, coup, load_sem,
         zbuf, field, ybuf, xcat, qt, q, a2, vloc, gmat, csc,
         expand, pattern, owner, rows_bf,
         part_send, part_recv, coef_send, coef_recv, halo_send, halo_recv,
         hsend_sem, hrecv_sem, psend_sem, precv_sem, csend_sem, crecv_sem):
    ngx, ngy, ngz = sizes
    ix, iy, iz = lax.axis_index("gx"), lax.axis_index("gy"), lax.axis_index("gz")
    cap = POS // ngz
    own = coup.shape[2] // ngz
    chunk = cap * SLOT

    def exists(d, sign):
        ok = None
        for pos, size, step in ((ix, ngx, d[0]), (iy, ngy, d[1]), (iz, ngz, d[2])):
            if step == 0:
                continue
            c = (pos + 1 < size) if step * sign > 0 else (pos > 0)
            ok = c if ok is None else jnp.logical_and(ok, c)
        return ok

    def target(d):
        return (ix + d[0], iy + d[1], iz + d[2])

    def peer(k):
        return lax.rem(iz + k, ngz)

    halo_recv[...] = jnp.zeros(halo_recv.shape, BF)
    barrier = pltpu.get_barrier_semaphore()
    for d in DIRS:
        @pl.when(exists(d, 1))
        def _(d=d):
            pl.semaphore_signal(barrier, inc=1, device_id=target(d), device_id_type=MESH)

    def greet(k, carry):
        pl.semaphore_signal(barrier, inc=1, device_id=(ix, iy, peer(k)), device_id_type=MESH)
        return carry

    lax.fori_loop(1, ngz, greet, 0)

    def span(pos, size):
        return 1 + (pos > 0).astype(jnp.int32) + (pos + 1 < size).astype(jnp.int32)

    n_greet = span(ix, ngx) * span(iy, ngy) * span(iz, ngz) - 1 + ngz - 1

    loads = [
        pltpu.make_async_copy(src, dst, load_sem.at[k])
        for k, (src, dst) in enumerate((
            (parts_in, parts), (amat_in, amat), (pot_in, pot), (atoms_in, atoms),
            (cells_in, cells), (coup_in, coup), (proj_in, proj)))]
    for load in loads:
        load.start()

    zero8 = jnp.zeros((SUB, LANES), F32)
    field[FIELD:, :] = jnp.zeros((TALL - FIELD, LANES), F32)
    ybuf[...] = jnp.zeros(ybuf.shape, F32)
    loads[0].wait()

    def take(u, carry):
        for v in range(WIDE):
            at = pl.multiple_of(u * ROW, SUB) + v * SUB
            tile = jnp.concatenate([parts[u, v], jnp.zeros((1, LANES), F32)], axis=0)
            field[pl.ds(at, SUB), :] = tile
        return carry

    lax.fori_loop(0, WIDE, take, 0)

    def halo_copy(d, slot):
        source = (d[0], d[1], 0) if d in CORNERS else d
        n = region_rows(d)
        k = DIRS.index(d)
        return pltpu.make_async_remote_copy(
            src_ref=halo_send.at[pl.ds(OFFSET[source], n)],
            dst_ref=halo_recv.at[slot, pl.ds(OFFSET[d], n)],
            send_sem=hsend_sem.at[k],
            recv_sem=hrecv_sem.at[slot, k],
            device_id=target(d),
            device_id_type=MESH,
        )

    def pack():
        def put(d, value):
            halo_send[pl.ds(OFFSET[d], region_rows(d)), :] = value.astype(BF)

        for d in XY:
            at = side(d[0], WIDE - 1) * ROW + side(d[1], WIDE - 1) * SUB
            put(d, jnp.concatenate([field[pl.ds(at, SUB), :], zero8], axis=0))
        for d in FACES:
            if d[0] != 0:
                at = side(d[0], WIDE - 1) * ROW
                put(d, jnp.concatenate([field[pl.ds(at, ROW), :], zero8], axis=0))
            elif d[1] != 0:
                v = side(d[1], WIDE - 1)
                value = jnp.concatenate(
                    [field[pl.ds(u * ROW + v * SUB, SUB), :] for u in range(WIDE)], axis=0)
                ybuf[pl.ds(side(d[1], 1) * LANES, ROW), :] = value
                put(d, jnp.concatenate([value, zero8], axis=0))
            else:
                put(d, field[pl.ds(side(d[2], ORDER), 176, stride=SUB), :])
        for d in YZ:
            put(d, ybuf[pl.ds(side(d[1], 1) * LANES + side(d[2], ORDER), 16, stride=SUB), :])
        for d in XZ:
            at = side(d[0], WIDE - 1) * ROW + side(d[2], ORDER)
            put(d, field[pl.ds(at, 16, stride=SUB), :])

    def halo_start(slot):
        for d in DIRS:
            @pl.when(exists(d, 1))
            def _(d=d):
                halo_copy(d, slot).start()

    def halo_wait(slot):
        for d in DIRS:
            @pl.when(exists(d, -1))
            def _(d=d):
                halo_copy(d, slot).wait_recv()
        for d in DIRS:
            @pl.when(exists(d, 1))
            def _(d=d):
                halo_copy(d, slot).wait_send()

    def unpack(slot):
        def got(d):
            return halo_recv[slot, pl.ds(OFFSET[d], region_rows(d)), :].astype(F32)

        def other(step, last):
            return 0 if step > 0 else last

        keep = iota((16, LANES), 0) < WIDE
        for d in FACES:
            if d[0] != 0:
                at = pl.ds(other(d[0], WIDE - 1) * ROW, ROW)
                field[at, :] = field[at, :] + got(d)[:ROW]
            elif d[1] != 0:
                v = other(d[1], WIDE - 1)
                ybuf[pl.ds(0, ROW), :] = got(d)[:ROW]
                for dz in (-1, 1):
                    rows = pl.ds(other(dz, ORDER), 16, stride=SUB)
                    ybuf[rows, :] = ybuf[rows, :] + got((0, d[1], dz))
                for u in range(WIDE):
                    at = pl.ds(u * ROW + v * SUB, SUB)
                    field[at, :] = field[at, :] + ybuf[pl.ds(u * SUB, SUB), :]
            else:
                rows = pl.ds(other(d[2], ORDER), 176, stride=SUB)
                field[rows, :] = field[rows, :] + got(d)
        for d in XZ:
            rows = pl.ds(other(d[0], WIDE - 1) * ROW + other(d[2], ORDER), 16, stride=SUB)
            field[rows, :] = field[rows, :] + jnp.where(keep, got(d), 0.0)
        for d in XY:
            base = other(d[0], WIDE - 1) * ROW + other(d[1], WIDE - 1) * SUB
            at = pl.ds(base, SUB)
            total = field[at, :] + got(d)[:SUB]
            field[at, :] = total
            first = got((d[0], d[1], 1))[ORDER:EDGE]
            last = got((d[0], d[1], -1))[:1]
            field[pl.ds(base, 1), :] = field[pl.ds(base, 1), :] + first
            field[pl.ds(base + ORDER, 1), :] = field[pl.ds(base + ORDER, 1), :] + last

    def split_cells(values):
        xs = []
        for p in range(2):
            for r in range(2):
                pieces = [
                    values[(ORDER * p + a) * ROW + ORDER * SUB * r:
                           (ORDER * p + a) * ROW + ORDER * SUB * r + EDGE * SUB]
                    for a in range(EDGE)]
                xs.append(jnp.concatenate(pieces + [zero8], axis=0))
        return xs

    def join_cells(blocks):
        rows = []
        for u in range(WIDE):
            halves = []
            for r in range(2):
                value = None
                for p in range(2):
                    a = u - ORDER * p
                    if 0 <= a <= ORDER:
                        piece = blocks[2 * p + r][a * EDGE * SUB:(a + 1) * EDGE * SUB]
                        value = piece if value is None else value + piece
                halves.append(value)
            left, right = halves
            cut = ORDER * SUB
            rows.append(jnp.concatenate(
                [left[:cut], left[cut:] + right[:SUB], right[SUB:]], axis=0))
        return rows

    pack()

    r_i, n_i = iota((KPAD, NODES), 0), iota((KPAD, NODES), 1)
    expand[...] = onehot(jnp.logical_and(
        jnp.logical_and(r_i < EDGE * EDGE * SUB, (r_i & 7) < EDGE),
        n_i == (r_i >> 3) * EDGE + (r_i & 7)))
    for load in loads[1:]:
        load.wait()
    a2[...] = dot_nt(dot(expand[:CROWS, :], amat[...]).astype(BF), expand[...]).astype(BF)

    vloc[...] = jnp.zeros(vloc.shape, F32)
    for g in range(CELLS):
        row = pot[g // 2, g % 2]
        high = row.astype(BF)
        low = (row - high.astype(F32)).astype(BF)
        block = sum(
            dot_nt(expand[:CROWS, :], jnp.broadcast_to(part, (LANES, NODES)))
            for part in (high, low))
        for a in range(EDGE):
            at = pl.ds((ORDER * (g // 2) + a) * ROW + ORDER * SUB * (g % 2), EDGE * SUB)
            vloc[at, :] = vloc[at, :] + block[a * EDGE * SUB:(a + 1) * EDGE * SUB]

    width = POS * BLK * PA
    s_i, col = iota((POS, width), 0), iota((POS, width), 1)
    in_slot = onehot(jnp.logical_and(col >= s_i * (BLK * PA), col < (s_i + 1) * (BLK * PA)))
    atom_bf = atoms[...].astype(F32).astype(BF)
    atom_all = dot(atom_bf, in_slot)
    atom_col = jnp.sum(jnp.where(iota((ngz, width), 0) == iz, atom_all, 0.0),
                       axis=0, keepdims=True)
    cell_all = dot(cells[...].astype(F32).astype(BF), in_slot)
    b_i, c_i = iota((BLK, width), 0), iota((BLK, width), 1)
    slot_of = ((c_i >> 4) * 43691) >> 17
    block_of = (((c_i - slot_of * (BLK * PA)) >> 2) * 43691) >> 17
    cell_col = jnp.sum(jnp.where(b_i == block_of, cell_all, 0.0), axis=0, keepdims=True)
    owner[...] = jnp.broadcast_to(
        jnp.where(atom_col >= 0.0, cell_col, -1.0), owner.shape)

    pr, pc = iota((KPAD, PGROUP), 0), iota((KPAD, PGROUP), 1)
    base = ((pr >> 4) & 7) * (BLK * PA) + (pr & 15)
    hit = pc == base
    for b in range(1, BLK):
        hit = jnp.logical_or(hit, pc == base + b * PA)
    pattern[...] = onehot(jnp.logical_and(hit, (pr & 15) < PA))

    pl.semaphore_wait(barrier, n_greet)
    halo_start(0)

    def merge(k, carry):
        columns = pl.ds(pl.multiple_of(k * PGROUP, LANES), PGROUP)
        rows_bf[...] = dot(expand[...], proj[:, columns]).astype(BF)
        cell_g = (iota((KPAD, PGROUP), 0) >> 7).astype(F32)
        chosen = jnp.where(jnp.broadcast_to(owner[0:1, columns], (KPAD, PGROUP)) == cell_g,
                           pattern[...].astype(F32), 0.0).astype(BF)
        tall = dot_nt(chosen, rows_bf[...]).astype(BF)
        wide = dot_nt(rows_bf[:CROWS, :], chosen).astype(BF)
        to = pl.ds(pl.multiple_of(k * GROUP, GROUP), GROUP)
        for g in range(CELLS):
            qt[to, g * KPAD:(g + 1) * KPAD] = tall[g * GROUP:(g + 1) * GROUP]
            q[g * CROWS:(g + 1) * CROWS, to] = wide[:, g * GROUP:(g + 1) * GROUP]
        return carry

    lax.fori_loop(0, POS // 8, merge, 0)

    at_s, at_c = iota((POS, COLS), 0), iota((POS, COLS), 1)
    j_c = (at_c >> 4) & (cap - 1)
    got_atoms = dot(atom_bf, onehot(at_s == iz * cap + j_c))
    k_r, k_c = iota((ngz, COLS), 0), iota((ngz, COLS), 1)
    here = jnp.logical_and(k_c >= k_r * chunk, k_c < (k_r + 1) * chunk)
    atom_row = jnp.sum(jnp.where(here, got_atoms, 0.0), axis=0, keepdims=True)
    m_r, m_c = iota((LANES, COLS), 0), iota((LANES, COLS), 1)
    same = jnp.logical_and((m_r >> 3) == (m_c & 15), (m_r >> 3) < PA)
    number = (m_r & 7).astype(F32)
    base_atom = (iz * own).astype(F32)
    member = onehot(jnp.logical_and(
        same, jnp.broadcast_to(atom_row, (LANES, COLS)) - base_atom == number))
    member_t = dot_nt(onehot(iota((COLS, COLS), 0) == iota((COLS, COLS), 1)),
                      member).astype(BF)
    atoms_here = coup.shape[2]
    pick = onehot(iota((SUB, atoms_here), 1) == iz * own + iota((SUB, atoms_here), 0))
    c_r, c_c = iota((LANES, LANES), 0), iota((LANES, LANES), 1)
    spread = onehot(jnp.logical_and(c_r == (c_c >> 3), (c_c >> 3) < PA))
    diagonal = (c_r & 7) == (c_c & 7)
    csc[...] = jnp.zeros(csc.shape, F32)
    for h in range(2):
        for t in range(PA):
            part = coup[t]
            high = part.astype(BF)
            if h:
                high = (part - high.astype(F32)).astype(BF)
            csc[t * SUB:(t + 1) * SUB, 0:PA] = dot_nt(pick, high)
        block = jnp.where(diagonal, dot(csc[...].astype(BF), spread), 0.0).astype(BF)
        gmat[h] = dot(dot(member_t, block).astype(BF), member).astype(BF)

    xcat[CROWS:, :] = jnp.zeros((KPAD - CROWS, CELLS * LANES), BF)
    zbuf[1] = jnp.zeros((FIELD, LANES), F32)

    halo_wait(0)
    unpack(0)
    zbuf[0] = field[pl.ds(0, FIELD), :]
    for g, value in enumerate(split_cells(field[pl.ds(0, FIELD), :])):
        xcat[pl.ds(0, CROWS), pl.ds(g * LANES, LANES)] = value.astype(BF)

    def exchange(src, dst, send_sem, recv_sem, k):
        to = peer(k)
        return pltpu.make_async_remote_copy(
            src_ref=src.at[pl.ds(pl.multiple_of(to * chunk, chunk), chunk)],
            dst_ref=dst.at[pl.ds(pl.multiple_of(iz * chunk, chunk), chunk)],
            send_sem=send_sem.at[k],
            recv_sem=recv_sem.at[k],
            device_id=(ix, iy, to),
            device_id_type=MESH,
        )

    def start_all(src, dst, send_sem, recv_sem):
        def go(k, carry):
            exchange(src, dst, send_sem, recv_sem, k).start()
            return carry

        lax.fori_loop(1, ngz, go, 0)
        mine = pl.ds(pl.multiple_of(iz * chunk, chunk), chunk)
        dst[mine, :] = src[mine, :]

    def wait_all(src, dst, send_sem, recv_sem):
        def go(k, carry):
            exchange(src, dst, send_sem, recv_sem, k).wait()
            return carry

        lax.fori_loop(1, ngz, go, 0)

    def step(t, carry):
        slot = lax.rem(t + 1, 2)
        now = lax.rem(t, 2)
        scale = jnp.where(t == 0, 1.0, 2.0) / half_width

        total = None
        for g in range(CELLS):
            term = dot(qt[:, g * KPAD:(g + 1) * KPAD], xcat[:, g * LANES:(g + 1) * LANES])
            total = term if total is None else total + term
        part_send[...] = total.astype(BF)
        start_all(part_send, part_recv, psend_sem, precv_sem)

        stiff = dot(a2[...], xcat[...])
        rows = join_cells([stiff[:, g * LANES:(g + 1) * LANES] for g in range(CELLS)])
        for u, row in enumerate(rows):
            at = pl.ds(u * ROW, ROW)
            field[at, :] = row + vloc[at, :] * zbuf[now, at, :]

        wait_all(part_send, part_recv, psend_sem, precv_sem)
        received = part_recv[...]
        coef_send[...] = (dot(gmat[0], received) + dot(gmat[1], received)).astype(BF)
        start_all(coef_send, coef_recv, csend_sem, crecv_sem)
        wait_all(coef_send, coef_recv, csend_sem, crecv_sem)

        coef = coef_recv[...]
        spread_cells = [dot(q[pl.ds(g * CROWS, CROWS), :], coef) for g in range(CELLS)]
        for u, row in enumerate(join_cells(spread_cells)):
            at = pl.ds(u * ROW, ROW)
            field[at, :] = field[at, :] + row

        pack()
        halo_start(slot)
        halo_wait(slot)
        unpack(slot)
        new = (field[pl.ds(0, FIELD), :] - center_value * zbuf[now]) * scale - zbuf[slot]
        zbuf[slot] = new
        for g, value in enumerate(split_cells(new)):
            xcat[pl.ds(0, CROWS), pl.ds(g * LANES, LANES)] = value.astype(BF)
        return carry

    lax.fori_loop(0, STEPS, step, 0)

    def give(u, carry):
        for v in range(WIDE):
            at = pl.multiple_of(u * ROW, SUB) + v * SUB
            out[u, v] = zbuf[STEPS % 2, pl.ds(at, SUB), :][:EDGE]
        return carry

    lax.fori_loop(0, WIDE, give, 0)


def local(sizes, parts, cell_matrix, cell_potential, projectors, slot_atom, slot_cells, coupling):
    ngz = sizes[2]

    def kernel(*refs):
        body(sizes, *refs)

    args = (
        parts,
        cell_matrix,
        jnp.transpose(cell_potential, (1, 2, 3, 0)),
        projectors.reshape(NODES, POS * BLK * PA),
        slot_atom.reshape(ngz, POS),
        jnp.transpose(slot_cells.reshape(POS, BLK)),
        jnp.transpose(coupling, (1, 2, 0)),
    )
    vm = pltpu.VMEM
    dma = pltpu.SemaphoreType.DMA
    n = len(DIRS)
    return pl.pallas_call(
        kernel,
        out_shape=jax.ShapeDtypeStruct(parts.shape, F32),
        in_specs=[pl.BlockSpec(memory_space=pl.ANY)] * 7,
        out_specs=pl.BlockSpec(memory_space=pltpu.VMEM),
        scratch_shapes=[vm(a.shape, a.dtype) for a in args] + [
            dma((7,)),
            vm((2, FIELD, LANES), F32),
            vm((TALL, LANES), F32),
            vm((2 * LANES, LANES), F32),
            vm((KPAD, CELLS * LANES), BF),
            vm((COLS, CELLS * KPAD), BF),
            vm((CELLS * CROWS, COLS), BF),
            vm((CROWS, KPAD), BF),
            vm((FIELD, LANES), F32),
            vm((2, COLS, COLS), BF),
            vm((LANES, LANES), F32),
            vm((KPAD, NODES), BF),
            vm((KPAD, PGROUP), BF),
            vm((SUB, POS * BLK * PA), F32),
            vm((KPAD, PGROUP), BF),
            vm((COLS, LANES), BF),
            vm((COLS, LANES), BF),
            vm((COLS, LANES), BF),
            vm((COLS, LANES), BF),
            vm((HALO_ROWS, LANES), BF),
            vm((2, HALO_ROWS, LANES), BF),
            dma((n,)),
            dma((2, n)),
            dma((ngz,)),
            dma((ngz,)),
            dma((ngz,)),
            dma((ngz,)),
        ],
        compiler_params=pltpu.CompilerParams(
            collective_id=0, has_side_effects=True, vmem_limit_bytes=56 * 1024 * 1024),
    )(*args)


def solution(mesh):
    sizes = tuple(mesh.shape[a] for a in ("gx", "gy", "gz"))

    def run(*args):
        return local(sizes, *args)

    in_specs = (
        P("gx", "gy", "gz", None),
        P(),
        P(None, "gx", "gy", "gz"),
        P("gx", "gy", "gz", None, None),
        P("gx", "gy", None, None),
        P("gx", "gy", "gz", None, None),
        P(("gx", "gy"), None, None),
    )
    out_specs = P("gx", "gy", "gz", None)
    return jax.shard_map(run, mesh=mesh, in_specs=in_specs, out_specs=out_specs, check_vma=False)
```
